512 devices in a mesh: dom: 64 (over x, z), rep: 8 (over y, core).
Axes of the slice: x: 4, y: 4, z: 16, core: 2. Of those that a mesh axis runs over, the one named last changes fastest.
Arguments:
- features: bfloat16 [65536, 256], P(('dom', 'rep')), may hold values from -6 to 6
- block_values: bfloat16 [512, 16, 8, 128, 128], P(('dom', 'rep'))
- block_columns: int32 [512, 16, 8], P(('dom', 'rep')), may hold values from 0 to 63, as said below
- weight: bfloat16 [256, 256], replicated, may hold values from -0.375 to 0.375
- cotangent: bfloat16 [65536, 256], P(('dom', 'rep')), may hold values from -6 to 6
Outputs:
- feature_grad: bfloat16 [65536, 256], P(('dom', 'rep'))
- weight_grad: float32 [256, 256], replicated
The draws below stay inside these ranges and needn't reach their ends.
Inputs may be any that keep to these rules, and one draw needn't show every extreme that they name: Slot (t, a) of the device with dom index d and rep index r lies at block row d * 8 + a and block column block_columns * 8 + r. The adjacency is symmetric: each slot at block row p and block column q has a partner slot of the same t at block row q and block column p whose block_values are its transpose; a slot with p equal to q holds a symmetric block.
All inputs are finite; a program needn't handle non-finite values.
Results may differ from the reference program's by a relative error of at most 0.006.
Values may be sent and summed in bfloat16 or wider, within the bound.
No kernel may reach another device: no remote copies, remote signals or barrier semaphores. Data moves between devices by JAX's collectives and lax.ppermute only.
A program may use at most 64 MiB of HBM per device.

```python
import math
import jax
import jax.numpy as jnp
from jax import lax

F = 256
BLK = 128
ROUNDS = 16
NODES = 65536
N_DOM = 64
N_REP = 8


def sigma_table(key):
    round_keys = jax.random.split(jax.random.fold_in(key, 5), ROUNDS * N_REP * N_REP)

    def shuffle_one(one_key):
        return jax.random.permutation(one_key, N_DOM)
    shuffles = jax.vmap(shuffle_one)(round_keys).astype(jnp.int32).reshape(ROUNDS, N_REP, N_REP, N_DOM)
    inverse = jnp.argsort(shuffles, axis=-1, stable=True).astype(jnp.int32)
    shifts = jax.random.randint(jax.random.fold_in(key, 6), (ROUNDS, N_REP), 0, N_DOM, dtype=jnp.int32)
    dom_ids = jnp.arange(N_DOM, dtype=jnp.int32)
    mirror = (shifts[:, :, None] - dom_ids[None, None, :]) % N_DOM
    row_ids = jnp.arange(N_REP, dtype=jnp.int32)
    above_diag = (row_ids[:, None] < row_ids[None, :])[None, :, :, None]
    below_diag = (row_ids[:, None] > row_ids[None, :])[None, :, :, None]
    swapped = jnp.swapaxes(inverse, 1, 2)
    return jnp.where(above_diag, shuffles, jnp.where(below_diag, swapped, mirror[:, :, None, :]))


def column_table(key):
    return jnp.transpose(sigma_table(key), (3, 2, 0, 1))


def draw_block_columns(key, part):
    return column_table(key).reshape(N_DOM * N_REP, ROUNDS, N_REP).astype(jnp.int32)


def draw_block_values(key, part):
    columns = column_table(key)
    table_shape = columns.shape
    dom_ids = jnp.arange(N_DOM, dtype=jnp.int32)[:, None, None, None]
    rep_ids = jnp.arange(N_REP, dtype=jnp.int32)[None, :, None, None]
    round_ids = jnp.arange(ROUNDS, dtype=jnp.int32)[None, None, :, None]
    row_ids = jnp.arange(N_REP, dtype=jnp.int32)[None, None, None, :]
    row_block = dom_ids * N_REP + row_ids
    col_block = columns * N_REP + rep_ids
    low_block = jnp.minimum(row_block, col_block)
    high_block = jnp.maximum(row_block, col_block)
    pair_code = low_block * (N_DOM * N_REP) + high_block
    round_flat = jnp.broadcast_to(round_ids, table_shape).reshape(-1)
    code_flat = jnp.broadcast_to(pair_code, table_shape).reshape(-1)
    flip_flat = jnp.broadcast_to(row_block > col_block, table_shape).reshape(-1)
    diag_flat = jnp.broadcast_to(row_block == col_block, table_shape).reshape(-1)
    base_key = jax.random.fold_in(key, 9)

    def one_block(round_id, code, flipped, diagonal):
        block_key = jax.random.fold_in(jax.random.fold_in(base_key, round_id), code)
        drawn = jax.random.normal(block_key, (BLK, BLK), jnp.float32)
        turned = drawn.T
        return jnp.where(diagonal, (drawn + turned) * 0.7071067811865476, jnp.where(flipped, turned, drawn))
    blocks = jax.vmap(one_block)(round_flat, code_flat, flip_flat, diag_flat)
    value_scale = (ROUNDS * N_REP * BLK) ** (-0.5)
    return (blocks * value_scale).reshape(N_DOM * N_REP, ROUNDS, N_REP, BLK, BLK).astype(jnp.bfloat16)


def level_of(stream_key, dims, shards, low, top_value):
    loudness = 1.0
    for axis_at, shards_of in shards:
        heights = jax.random.uniform(jax.random.fold_in(jax.random.fold_in(stream_key, 6), axis_at), (shards_of,), jnp.float32, low / len(shards), top_value / len(shards))
        loudness = loudness * jnp.repeat(jnp.exp(heights), dims[axis_at] // shards_of).reshape((-1,) + (1,) * (len(dims) - 1 - axis_at))
    return loudness


def bell_draw(key, shape, deviation, limit, pieces=(), held_as=jnp.bfloat16):
    drawn = deviation * jax.random.normal(key, shape, jnp.float32)
    if pieces:
        drawn = drawn * level_of(key, shape, pieces, -0.22, 0.18)
    return jnp.clip(drawn, -limit, limit).astype(held_as)


def setup_inputs(seed: int = 0) -> dict:
    key_list = jax.random.split(jax.random.key(seed), 6)
    features = bell_draw(key_list[0], (NODES, F), 1.0, 6.0, ((0, 512),))
    block_values = draw_block_values(jax.random.fold_in(key_list[5], 71), 0)
    block_columns = draw_block_columns(jax.random.fold_in(key_list[5], 71), 0)
    weight = bell_draw(key_list[3], (F, F), F ** -0.5, 0.375)
    cotangent = bell_draw(key_list[4], (NODES, F), 1.0, 6.0, ((0, 512),))
    return {"features": features, "block_values": block_values, "block_columns": block_columns, "weight": weight, "cotangent": cotangent}


def apply_adjacency(node_field, values, columns):
    rep_ids = jnp.arange(N_REP, dtype=jnp.int32)

    def one_panel(operands):
        panel_values, panel_columns = operands
        picked = node_field[panel_columns, rep_ids[:, None, None]]
        return jnp.einsum('rtaij,rtajf->aif', panel_values.astype(jnp.float32), picked.astype(jnp.float32))
    result = lax.map(one_panel, (values, columns))
    return result.reshape(NODES, F)

def reference(features, block_values, block_columns, weight, cotangent):
    values = block_values.reshape(N_DOM, N_REP, ROUNDS, N_REP, BLK, BLK)
    columns = block_columns.reshape(N_DOM, N_REP, ROUNDS, N_REP)
    hidden = apply_adjacency(features.reshape(N_DOM, N_REP, BLK, F), values, columns).astype(jnp.bfloat16)
    pre_act = jnp.dot(hidden, weight, preferred_element_type=jnp.float32)
    sigmoid_value = jax.nn.sigmoid(pre_act)
    slope_value = sigmoid_value * (1.0 + pre_act * (1.0 - sigmoid_value))
    grad_pre = (cotangent.astype(jnp.float32) * slope_value).astype(jnp.bfloat16)
    weight_grad = jnp.dot(hidden.T, grad_pre, preferred_element_type=jnp.float32) * (1.0 / math.sqrt(NODES))
    hidden_grad = jnp.dot(grad_pre, weight.T, preferred_element_type=jnp.float32).astype(jnp.bfloat16)
    feature_grad = apply_adjacency(hidden_grad.reshape(N_DOM, N_REP, BLK, F), values, columns).astype(jnp.bfloat16)
    return (feature_grad, weight_grad)
```

```python
import math

import jax
import jax.numpy as jnp
from jax import lax
from jax.experimental import pallas as pl
from jax.experimental.pallas import tpu as pltpu
from jax.sharding import Mesh
from jax.sharding import PartitionSpec as P


AXES = ("X", "ZH", "ZL", "Y", "C")
DOM = ("X", "ZH", "ZL")
REP = ("Y", "C")
N_X, N_Z, FOUR = 4, 16, 4

PLACE = (0, 48, 4, 56, 16, 40, 20, 44, 60, 8, 52, 12, 32, 24, 36, 28)
PIECES = (16, 16, 16, 8, 8)


def spread(value, axes):
    copies = jnp.broadcast_to(value, (lax.axis_size(axes), *value.shape))
    return lax.all_to_all(copies, axes, 0, 0, tiled=True)


def shift(value, dx, dz):
    pairs = []
    for x in range(N_X):
        for z in range(N_Z):
            pairs.append(((x + dx) % N_X * N_Z + (z + dz) % N_Z, x * N_Z + z))
    return lax.ppermute(value, DOM, pairs)


def gather_panels(value):
    own = spread(value, "ZH")
    up = shift(own[:2], 0, 2)
    down = shift(own[2:], 0, -2)
    far_up = shift(own, 2, 1)
    far_down = shift(own, 2, -1)
    held = jnp.concatenate([own, up, down, far_up, far_down], axis=0)
    half = jnp.concatenate([own, far_up], axis=0)
    return (held, shift(held, 1, 0), shift(held, -1, 0), shift(half, 0, 1), shift(half, 0, -1))


def places(columns):
    cols = columns.T
    dx = (cols // N_Z - lax.axis_index("X")) % N_X
    dl = (cols - lax.axis_index("ZL")) % FOUR
    kind = dx * FOUR + dl
    base = jnp.zeros_like(cols)
    for k, start in enumerate(PLACE):
        base = jnp.where(kind == k, start, base)
    return base + cols // FOUR % FOUR


def product_kernel(place_ref, values_ref, *refs):
    pieces, (out_ref, panels, blocks, piece_sem, block_sem) = refs[:5], refs[5:]
    rows = out_ref.shape[0]
    rounds = blocks.shape[1]
    copies = []
    for a in range(rows):
        copies.append(pltpu.make_async_copy(values_ref.at[:, a], blocks.at[a], block_sem.at[a]))
    moves, at = [], 0
    for i, piece in enumerate(pieces):
        n = PIECES[i]
        moves.append(pltpu.make_async_copy(piece, panels.at[pl.ds(at, n)], piece_sem.at[i]))
        at += n
    for move in moves:
        move.start()
    for copy in copies:
        copy.start()
    for move in moves:
        move.wait()
    for a in range(rows):
        copies[a].wait()
        total = None
        for t in range(0, rounds, 2):
            left = jnp.concatenate([blocks[a, t], blocks[a, t + 1]], axis=1)
            right = jnp.concatenate(
                [panels[place_ref[a, t]], panels[place_ref[a, t + 1]]], axis=0
            )
            term = jnp.dot(left, right, preferred_element_type=jnp.float32)
            total = term if total is None else total + term
        out_ref[a] = total.astype(out_ref.dtype)


def panel_products(values, place, pieces):
    rounds, rows, blk, _ = values.shape
    width = pieces[0].shape[-1]
    any_space = pl.BlockSpec(memory_space=pl.ANY)
    return pl.pallas_call(
        product_kernel,
        out_shape=jax.ShapeDtypeStruct((rows, blk, width), jnp.bfloat16),
        in_specs=[pl.BlockSpec(memory_space=pltpu.SMEM), any_space] + [any_space] * 5,
        out_specs=pl.BlockSpec(memory_space=pltpu.VMEM),
        scratch_shapes=[
            pltpu.VMEM((sum(PIECES), blk, width), jnp.bfloat16),
            pltpu.VMEM((rows, rounds, blk, blk), jnp.bfloat16),
            pltpu.SemaphoreType.DMA((5,)),
            pltpu.SemaphoreType.DMA((rows,)),
        ],
        compiler_params=pltpu.CompilerParams(vmem_limit_bytes=24 * 2**20),
        cost_estimate=pl.CostEstimate(
            flops=2 * rounds * rows * blk * blk * width, bytes_accessed=9 * 2**20, transcendentals=0
        ),
        name="panel_products",
    )(place, values, *pieces)


def summed_over_rep(partial):
    received = lax.all_to_all(partial, REP, 0, 0, tiled=True)
    return jnp.sum(received.astype(jnp.float32), axis=0)


def dense_grads(hidden, weight, cotangent):
    pre_act = jnp.dot(hidden, weight, preferred_element_type=jnp.float32)
    sigmoid_value = jax.nn.sigmoid(pre_act)
    slope_value = sigmoid_value * (1.0 + pre_act * (1.0 - sigmoid_value))
    grad_pre = (cotangent.astype(jnp.float32) * slope_value).astype(jnp.bfloat16)
    hidden_grad = jnp.einsum(
        "rg,fg->rf", grad_pre, weight, preferred_element_type=jnp.float32
    ).astype(jnp.bfloat16)
    weight_part = jnp.einsum("rf,rg->fg", hidden, grad_pre, preferred_element_type=jnp.float32)
    return hidden_grad, weight_part


def summed_weight(part):
    near, far = ("ZH", "Y", "C"), ("X", "ZL")
    f = part.shape[1]
    n = lax.axis_size(near)
    pieces = lax.all_to_all(part.reshape(n, -1, f), near, 0, 0, tiled=True)
    own = jnp.sum(pieces, axis=0)
    own = jnp.sum(spread(own, far), axis=0)
    return spread(own, near).reshape(part.shape)


def shards(features, block_values, block_columns, weight, cotangent):
    values = block_values[0]
    node_total = features.shape[0] * lax.axis_size(AXES)
    inv_scale = 1.0 / math.sqrt(node_total)
    place = places(block_columns[0])
    partial = panel_products(values, place, gather_panels(features))
    hidden = summed_over_rep(partial).astype(jnp.bfloat16)
    hidden_grad, weight_part = dense_grads(hidden, weight, cotangent)
    weight_grad = summed_weight(weight_part) * inv_scale
    back = panel_products(values, place, gather_panels(hidden_grad))
    feature_grad = summed_over_rep(back).astype(jnp.bfloat16)
    return feature_grad, weight_grad


def solution(mesh):
    finer = Mesh(mesh.devices.reshape(4, 4, 4, 4, 2), AXES)
    in_specs = (
        P(AXES, None),
        P(AXES, None, None, None, None),
        P(AXES, None, None),
        P(),
        P(AXES, None),
    )
    out_specs = (P(AXES, None), P())
    return jax.shard_map(
        shards, mesh=finer, in_specs=in_specs, out_specs=out_specs, check_vma=False
    )
```

```python
import math

import jax
import jax.numpy as jnp
from jax import lax
from jax.experimental import pallas as pl
from jax.experimental.pallas import tpu as pltpu
from jax.sharding import Mesh
from jax.sharding import PartitionSpec as P


AXES = ("X", "ZH", "ZL", "Y", "C")
DOM = ("X", "ZH", "ZL")
REP = ("Y", "C")
N_X, N_Z, FOUR = 4, 16, 4

SECOND = (((0, 2), (2, 1), (2, -1)), ((2, 0), (1, 2), (-1, -2)))
THIRD = (((1, 0), (-1, 0), (0, 1), (0, -1)), ((0, 1), (0, -1), (1, 0), (-1, 0)))
PIECES = (16, 16, 16, 8, 8)
BLK = 128


def place_table(core):
    held = ((0, 0),) + SECOND[core]
    table = {k: 4 * i for i, k in enumerate(held)}
    at = PIECES[0]
    for i, (dx, dz) in enumerate(THIRD[core]):
        sent = held if i < 2 else (held[0], held[2])
        for hx, hz in sent:
            table[(hx + dx, hz + dz)] = at
            at += 4
    flat = [None] * (N_X * FOUR)
    for (dx, dl), start in table.items():
        flat[dx % N_X * FOUR + dl % FOUR] = start
    return flat


def spread(value, axes):
    copies = jnp.broadcast_to(value, (lax.axis_size(axes), *value.shape))
    return lax.all_to_all(copies, axes, 0, 0, tiled=True)


def shift(value, first, second):
    pairs = []
    for x in range(N_X):
        for z in range(N_Z):
            for core, (dx, dz) in enumerate((first, second)):
                source = (x + dx) % N_X * N_Z + (z + dz) % N_Z
                pairs.append((source * 2 + core, (x * N_Z + z) * 2 + core))
    return lax.ppermute(value, DOM + ("C",), pairs)


def halves(value):
    high = lax.reduce_precision(value, 8, 7)
    low = lax.reduce_precision(value - high, 8, 7)
    return jnp.concatenate([high, low], axis=-2).astype(jnp.bfloat16)


def whole(pair):
    high, low = jnp.split(pair.astype(jnp.float32), 2, axis=-2)
    return high + low


def gather_panels(value, riding=None):
    rows, width = value.shape

    def stacked(parts, pair):
        return jnp.concatenate(parts if pair is None else [*parts, pair], axis=0)

    pair = None if riding is None else halves(riding)
    got = spread(stacked([value], pair), "ZH")
    own = got[:, :rows].reshape(-1, width)
    size = own.shape[0]
    if riding is not None:
        pair = halves(jnp.sum(whole(got[:, rows:]), axis=0))
    packed = stacked([own], pair)
    more = [shift(packed, *steps) for steps in zip(*SECOND)]
    if riding is not None:
        terms = [whole(pair)] + [whole(m[size:]) for m in more]
        pair = halves((terms[0] + terms[1]) + (terms[2] + terms[3]))
    held = stacked([own] + [m[:size] for m in more], pair)
    half = stacked([own, more[1][:size]], pair)
    near = [shift(v, *steps) for v, steps in zip((held, held, half, half), zip(*THIRD))]
    total = None
    if riding is not None:
        n = pair.shape[0]
        plus, minus, side = (whole(near[i][-n:]) for i in range(3))
        total = (whole(pair) + side) + (plus + minus)
    return (held, *near), total


def places(columns):
    cols = columns.T
    dx = (cols // N_Z - lax.axis_index("X")) % N_X
    dl = (cols - lax.axis_index("ZL")) % FOUR
    kind = dx * FOUR + dl
    core = lax.axis_index("C")
    base = jnp.zeros_like(cols)
    for k, (zero, one) in enumerate(zip(place_table(0), place_table(1))):
        base = jnp.where(kind == k, jnp.where(core == 0, zero, one), base)
    return (base + cols // FOUR % FOUR) * BLK


def product_kernel(place_ref, values_ref, *refs):
    pieces, (out_ref, panels, blocks, piece_sem, block_sem) = refs[:5], refs[5:]
    rows, rounds, blk, _ = blocks.shape
    copies = []
    for a in range(rows):
        copies.append(pltpu.make_async_copy(values_ref.at[:, a], blocks.at[a], block_sem.at[a]))
    moves, at = [], 0
    for i, piece in enumerate(pieces):
        n = PIECES[i] * blk
        moves.append(
            pltpu.make_async_copy(
                piece.at[pl.ds(0, n)], panels.at[pl.ds(at, n)], piece_sem.at[i]
            )
        )
        at += n
    for move in moves:
        move.start()
    for copy in copies:
        copy.start()
    for move in moves:
        move.wait()

    def panel(a, t):
        return panels[pl.ds(pl.multiple_of(place_ref[a, t], blk), blk)]

    for a in range(rows):
        copies[a].wait()
        total = None
        for t in range(0, rounds, 2):
            left = jnp.concatenate([blocks[a, t], blocks[a, t + 1]], axis=1)
            right = jnp.concatenate([panel(a, t), panel(a, t + 1)], axis=0)
            term = jnp.dot(left, right, preferred_element_type=jnp.float32)
            total = term if total is None else total + term
        out_ref[a, 0:blk] = total.astype(out_ref.dtype)


def panel_products(values, place, pieces, spare=0):
    rounds, rows, blk, _ = values.shape
    width = pieces[0].shape[-1]
    any_space = pl.BlockSpec(memory_space=pl.ANY)
    return pl.pallas_call(
        product_kernel,
        out_shape=jax.ShapeDtypeStruct((rows, blk + spare, width), jnp.bfloat16),
        in_specs=[
            pl.BlockSpec(memory_space=pltpu.SMEM),
            pl.BlockSpec(memory_space=pltpu.HBM),
        ]
        + [any_space] * 5,
        out_specs=pl.BlockSpec(memory_space=pltpu.VMEM),
        scratch_shapes=[
            pltpu.VMEM((sum(PIECES) * blk, width), jnp.bfloat16),
            pltpu.VMEM((rows, rounds, blk, blk), jnp.bfloat16),
            pltpu.SemaphoreType.DMA((5,)),
            pltpu.SemaphoreType.DMA((rows,)),
        ],
        compiler_params=pltpu.CompilerParams(vmem_limit_bytes=24 * 2**20),
        cost_estimate=pl.CostEstimate(
            flops=2 * rounds * rows * blk * blk * width, bytes_accessed=9 * 2**20, transcendentals=0
        ),
        name="panel_products",
    )(place, values, *pieces)


def summed_over_rep(partial):
    received = lax.all_to_all(partial, REP, 0, 0, tiled=True)
    return jnp.sum(received.astype(jnp.float32), axis=0)


def dense_grads(hidden, weight, cotangent):
    pre_act = jnp.dot(hidden, weight, preferred_element_type=jnp.float32)
    sigmoid_value = jax.nn.sigmoid(pre_act)
    slope_value = sigmoid_value * (1.0 + pre_act * (1.0 - sigmoid_value))
    grad_pre = (cotangent.astype(jnp.float32) * slope_value).astype(jnp.bfloat16)
    hidden_grad = jnp.einsum(
        "rg,fg->rf", grad_pre, weight, preferred_element_type=jnp.float32
    ).astype(jnp.bfloat16)
    weight_part = jnp.einsum("rf,rg->fg", hidden, grad_pre, preferred_element_type=jnp.float32)
    return hidden_grad, weight_part


def shards(features, block_values, block_columns, weight, cotangent):
    values = block_values[0]
    rows, f = features.shape
    node_total = rows * lax.axis_size(AXES)
    inv_scale = 1.0 / math.sqrt(node_total)
    place = places(block_columns[0])
    panels, _ = gather_panels(features)
    partial = panel_products(values, place, panels)
    hidden = summed_over_rep(partial).astype(jnp.bfloat16)
    hidden_grad, weight_part = dense_grads(hidden, weight, cotangent)
    n_rep = lax.axis_size(REP)
    slices = lax.all_to_all(weight_part.reshape(n_rep, -1, f), REP, 0, 0, tiled=True)
    panels, weight_slice = gather_panels(hidden_grad, jnp.sum(slices, axis=0))
    extra = weight_slice.shape[0]
    back = panel_products(values, place, panels, extra)
    back = back.at[:, rows:].set(weight_slice.astype(jnp.bfloat16)[None])
    received = lax.all_to_all(back, REP, 0, 0, tiled=True).astype(jnp.float32)
    feature_grad = jnp.sum(received[:, :rows], axis=0).astype(jnp.bfloat16)
    weight_grad = received[:, rows:].reshape(f, f) * inv_scale
    return feature_grad, weight_grad


def solution(mesh):
    finer = Mesh(mesh.devices.reshape(4, 4, 4, 4, 2), AXES)
    in_specs = (
        P(AXES, None),
        P(AXES, None, None, None, None),
        P(AXES, None, None),
        P(),
        P(AXES, None),
    )
    out_specs = (P(AXES, None), P())
    return jax.shard_map(
        shards, mesh=finer, in_specs=in_specs, out_specs=out_specs, check_vma=False
    )
```

```python
import math

import jax
import jax.numpy as jnp
from jax import lax
from jax.experimental import pallas as pl
from jax.experimental.pallas import tpu as pltpu
from jax.sharding import Mesh
from jax.sharding import PartitionSpec as P


AXES = ("X", "ZH", "ZL", "Y", "C")
DOM = ("X", "ZH", "ZL")
REP = ("Y", "C")
N_X, N_Z, FOUR = 4, 16, 4

SECOND = (((0, 2), (2, 1), (2, -1)), ((2, 0), (1, 2), (-1, -2)))
THIRD = (((1, 0), (-1, 0), (0, 1), (0, -1)), ((0, 1), (0, -1), (1, 0), (-1, 0)))
PIECES = (16, 16, 16, 8, 8)
BLK = 128


def place_table(core):
    held = ((0, 0),) + SECOND[core]
    table = {k: 4 * i for i, k in enumerate(held)}
    at = PIECES[0]
    for i, (dx, dz) in enumerate(THIRD[core]):
        sent = held if i < 2 else (held[0], held[2])
        for hx, hz in sent:
            table[(hx + dx, hz + dz)] = at
            at += 4
    flat = [None] * (N_X * FOUR)
    for (dx, dl), start in table.items():
        flat[dx % N_X * FOUR + dl % FOUR] = start
    return flat


def spread(value, axes):
    copies = jnp.broadcast_to(value, (lax.axis_size(axes), *value.shape))
    return lax.all_to_all(copies, axes, 0, 0, tiled=True)


def shift(value, first, second):
    pairs = []
    for x in range(N_X):
        for z in range(N_Z):
            for core, (dx, dz) in enumerate((first, second)):
                if (dx, dz) == (0, 2) and z % 2:
                    dz = -2
                source = (x + dx) % N_X * N_Z + (z + dz) % N_Z
                pairs.append((source * 2 + core, (x * N_Z + z) * 2 + core))
    return lax.ppermute(value, DOM + ("C",), pairs)


def halves(value):
    high = lax.reduce_precision(value, 8, 7)
    low = lax.reduce_precision(value - high, 8, 7)
    return jnp.concatenate([high, low], axis=-2).astype(jnp.bfloat16)


def whole(pair):
    high, low = jnp.split(pair.astype(jnp.float32), 2, axis=-2)
    return high + low


def gather_panels(value, riding=None):
    rows, width = value.shape

    def stacked(parts, pair):
        return jnp.concatenate(parts if pair is None else [*parts, pair], axis=0)

    got = spread(stacked([value], riding), "ZH")
    own = got[:, :rows].reshape(-1, width)
    size, pair = own.shape[0], None
    if riding is not None:
        pair = halves(jnp.sum(got[:, rows:].astype(jnp.float32), axis=0))
    packed = stacked([own], pair)
    more = [shift(packed, *steps) for steps in zip(*SECOND)]
    if riding is not None:
        terms = [whole(pair)] + [whole(m[size:]) for m in more]
        pair = halves((terms[0] + terms[1]) + (terms[2] + terms[3]))
    held = stacked([own] + [m[:size] for m in more], pair)
    half = stacked([own, more[1][:size]], pair)
    near = [shift(v, *steps) for v, steps in zip((held, held, half, half), zip(*THIRD))]
    total = None
    if riding is not None:
        n = pair.shape[0]
        plus, minus, side = (whole(near[i][-n:]) for i in range(3))
        total = (whole(pair) + side) + (plus + minus)
    return (held, *near), total


def places(columns):
    cols = columns.T
    dx = (cols // N_Z - lax.axis_index("X")) % N_X
    dl = (cols - lax.axis_index("ZL")) % FOUR
    kind = dx * FOUR + dl
    core = lax.axis_index("C")
    base = jnp.zeros_like(cols)
    for k, (zero, one) in enumerate(zip(place_table(0), place_table(1))):
        base = jnp.where(kind == k, jnp.where(core == 0, zero, one), base)
    return (base + cols // FOUR % FOUR) * BLK


def product_kernel(place_ref, values_ref, *refs):
    pieces, (out_ref, panels, blocks, piece_sem, block_sem) = refs[:5], refs[5:]
    rows, rounds, blk, _ = blocks.shape
    copies = []
    for a in range(rows):
        copies.append(pltpu.make_async_copy(values_ref.at[:, a], blocks.at[a], block_sem.at[a]))
    moves, at = [], 0
    for i, piece in enumerate(pieces):
        n = PIECES[i] * blk
        moves.append(
            pltpu.make_async_copy(
                piece.at[pl.ds(0, n)], panels.at[pl.ds(at, n)], piece_sem.at[i]
            )
        )
        at += n
    for move in moves:
        move.start()
    for copy in copies:
        copy.start()
    for move in moves:
        move.wait()

    def panel(a, t):
        return panels[pl.ds(pl.multiple_of(place_ref[a, t], blk), blk)]

    for a in range(rows):
        copies[a].wait()
        total = None
        for t in range(0, rounds, 2):
            left = jnp.concatenate([blocks[a, t], blocks[a, t + 1]], axis=1)
            right = jnp.concatenate([panel(a, t), panel(a, t + 1)], axis=0)
            term = jnp.dot(left, right, preferred_element_type=jnp.float32)
            total = term if total is None else total + term
        out_ref[a, 0:blk] = total.astype(out_ref.dtype)


def panel_products(values, place, pieces, spare=0):
    rounds, rows, blk, _ = values.shape
    width = pieces[0].shape[-1]
    any_space = pl.BlockSpec(memory_space=pl.ANY)
    return pl.pallas_call(
        product_kernel,
        out_shape=jax.ShapeDtypeStruct((rows, blk + spare, width), jnp.bfloat16),
        in_specs=[
            pl.BlockSpec(memory_space=pltpu.SMEM),
            pl.BlockSpec(memory_space=pltpu.HBM),
        ]
        + [any_space] * 5,
        out_specs=pl.BlockSpec(memory_space=pltpu.VMEM),
        scratch_shapes=[
            pltpu.VMEM((sum(PIECES) * blk, width), jnp.bfloat16),
            pltpu.VMEM((rows, rounds, blk, blk), jnp.bfloat16),
            pltpu.SemaphoreType.DMA((5,)),
            pltpu.SemaphoreType.DMA((rows,)),
        ],
        compiler_params=pltpu.CompilerParams(vmem_limit_bytes=24 * 2**20),
        cost_estimate=pl.CostEstimate(
            flops=2 * rounds * rows * blk * blk * width, bytes_accessed=9 * 2**20, transcendentals=0
        ),
        name="panel_products",
    )(place, pltpu.with_memory_space_constraint(values, pltpu.HBM), *pieces)


def summed_over_rep(partial):
    received = lax.all_to_all(partial, REP, 0, 0, tiled=True)
    return jnp.sum(received.astype(jnp.float32), axis=0)


def dense_grads(hidden, weight, cotangent):
    pre_act = jnp.dot(hidden, weight, preferred_element_type=jnp.float32)
    sigmoid_value = jax.nn.sigmoid(pre_act)
    slope_value = sigmoid_value * (1.0 + pre_act * (1.0 - sigmoid_value))
    grad_pre = (cotangent.astype(jnp.float32) * slope_value).astype(jnp.bfloat16)
    hidden_grad = jnp.einsum(
        "rg,fg->rf", grad_pre, weight, preferred_element_type=jnp.float32
    ).astype(jnp.bfloat16)
    weight_part = jnp.einsum("rf,rg->fg", hidden, grad_pre, preferred_element_type=jnp.float32)
    return hidden_grad, weight_part


def shards(features, block_values, block_columns, weight, cotangent):
    values = block_values[0]
    rows, f = features.shape
    node_total = rows * lax.axis_size(AXES)
    inv_scale = 1.0 / math.sqrt(node_total)
    place = places(block_columns[0])
    panels, _ = gather_panels(features)
    partial = panel_products(values, place, panels)
    hidden = summed_over_rep(partial).astype(jnp.bfloat16)
    hidden_grad, weight_part = dense_grads(hidden, weight, cotangent)
    n_rep = lax.axis_size(REP)
    slices = lax.all_to_all(weight_part.reshape(n_rep, -1, f), REP, 0, 0, tiled=True)
    panels, weight_slice = gather_panels(hidden_grad, jnp.sum(slices, axis=0).astype(jnp.bfloat16))
    extra = weight_slice.shape[0]
    back = panel_products(values, place, panels, extra)
    back = back.at[:, rows:].set(weight_slice.astype(jnp.bfloat16)[None])
    received = lax.all_to_all(back, REP, 0, 0, tiled=True).astype(jnp.float32)
    feature_grad = jnp.sum(received[:, :rows], axis=0).astype(jnp.bfloat16)
    weight_grad = received[:, rows:].reshape(f, f) * inv_scale
    return feature_grad, weight_grad


def solution(mesh):
    finer = Mesh(mesh.devices.reshape(4, 4, 4, 4, 2), AXES)
    in_specs = (
        P(AXES, None),
        P(AXES, None, None, None, None),
        P(AXES, None, None),
        P(),
        P(AXES, None),
    )
    out_specs = (P(AXES, None), P())
    return jax.shard_map(
        shards, mesh=finer, in_specs=in_specs, out_specs=out_specs, check_vma=False
    )
```

```python
import math

import jax
import jax.numpy as jnp
from jax import lax
from jax.experimental import pallas as pl
from jax.experimental.pallas import tpu as pltpu
from jax.sharding import Mesh
from jax.sharding import PartitionSpec as P


AXES = ("X", "ZH", "ZL", "Y", "C")
DOM = ("X", "ZH", "ZL")
REP = ("Y", "C")
N_X, N_Z, FOUR = 4, 16, 4

SECOND = (((0, 2), (2, 1), (2, -1)), ((2, 0), (1, 2), (-1, -2)))
THIRD = (((1, 0), (-1, 0), (0, 1), (0, -1)), ((0, 1), (0, -1), (1, 0), (-1, 0)))
PIECES = (16, 16, 16, 8, 8)
BLK = 128


def place_table(core):
    held = ((0, 0),) + SECOND[core]
    table = {k: 4 * i for i, k in enumerate(held)}
    at = PIECES[0]
    for i, (dx, dz) in enumerate(THIRD[core]):
        sent = held if i < 2 else (held[0], held[2])
        for hx, hz in sent:
            table[(hx + dx, hz + dz)] = at
            at += 4
    flat = [None] * (N_X * FOUR)
    for (dx, dl), start in table.items():
        flat[dx % N_X * FOUR + dl % FOUR] = start
    return flat


def shift(value, first, second):
    pairs = []
    for x in range(N_X):
        for z in range(N_Z):
            for core, (dx, dz) in enumerate((first, second)):
                if (dx, dz) == (0, 2) and z % 2:
                    dz = -2
                source = (x + dx) % N_X * N_Z + (z + dz) % N_Z
                pairs.append((source * 2 + core, (x * N_Z + z) * 2 + core))
    return lax.ppermute(value, DOM + ("C",), pairs)


def halves(value):
    high = lax.reduce_precision(value, 8, 7)
    low = lax.reduce_precision(value - high, 8, 7)
    return jnp.concatenate([high, low], axis=-2).astype(jnp.bfloat16)


def whole(pair):
    high, low = jnp.split(pair.astype(jnp.float32), 2, axis=-2)
    return high + low


def gather_panels(value, riding=None):
    rows, width = value.shape

    def stacked(parts, pair):
        return jnp.concatenate(parts if pair is None else [*parts, pair], axis=0)

    got = lax.all_gather(stacked([value], riding), "ZH", axis=0, tiled=False)
    own = got[:, :rows].reshape(-1, width)
    size, pair = own.shape[0], None
    if riding is not None:
        pair = halves(jnp.sum(got[:, rows:].astype(jnp.float32), axis=0))
    packed = stacked([own], pair)
    more = [shift(packed, *steps) for steps in zip(*SECOND)]
    if riding is not None:
        terms = [whole(pair)] + [whole(m[size:]) for m in more]
        pair = halves((terms[0] + terms[1]) + (terms[2] + terms[3]))
    held = stacked([own] + [m[:size] for m in more], pair)
    half = stacked([own, more[1][:size]], pair)
    near = [shift(v, *steps) for v, steps in zip((held, held, half, half), zip(*THIRD))]
    total = None
    if riding is not None:
        n = pair.shape[0]
        plus, minus, side = (whole(near[i][-n:]) for i in range(3))
        total = (whole(pair) + side) + (plus + minus)
    return (held, *near), total


def places(columns):
    cols = columns.T
    dx = (cols // N_Z - lax.axis_index("X")) % N_X
    dl = (cols - lax.axis_index("ZL")) % FOUR
    kind = dx * FOUR + dl
    core = lax.axis_index("C")
    base = jnp.zeros_like(cols)
    for k, (zero, one) in enumerate(zip(place_table(0), place_table(1))):
        base = jnp.where(kind == k, jnp.where(core == 0, zero, one), base)
    return (base + cols // FOUR % FOUR) * BLK


def product_kernel(place_ref, values_ref, *refs):
    pieces, (out_ref, panels, blocks, piece_sem, block_sem) = refs[:5], refs[5:]
    rows, rounds, blk, _ = blocks.shape
    copies = []
    for a in range(rows):
        copies.append(pltpu.make_async_copy(values_ref.at[:, a], blocks.at[a], block_sem.at[a]))
    moves, at = [], 0
    for i, piece in enumerate(pieces):
        n = PIECES[i] * blk
        moves.append(
            pltpu.make_async_copy(
                piece.at[pl.ds(0, n)], panels.at[pl.ds(at, n)], piece_sem.at[i]
            )
        )
        at += n
    for move in moves:
        move.start()
    for copy in copies:
        copy.start()
    for move in moves:
        move.wait()

    def panel(a, t):
        return panels[pl.ds(pl.multiple_of(place_ref[a, t], blk), blk)]

    for a in range(rows):
        copies[a].wait()
        total = None
        for t in range(0, rounds, 2):
            left = jnp.concatenate([blocks[a, t], blocks[a, t + 1]], axis=1)
            right = jnp.concatenate([panel(a, t), panel(a, t + 1)], axis=0)
            term = jnp.dot(left, right, preferred_element_type=jnp.float32)
            total = term if total is None else total + term
        out_ref[a, 0:blk] = total.astype(out_ref.dtype)


def panel_products(values, place, pieces, spare=0):
    rounds, rows, blk, _ = values.shape
    width = pieces[0].shape[-1]
    any_space = pl.BlockSpec(memory_space=pl.ANY)
    return pl.pallas_call(
        product_kernel,
        out_shape=jax.ShapeDtypeStruct((rows, blk + spare, width), jnp.bfloat16),
        in_specs=[
            pl.BlockSpec(memory_space=pltpu.SMEM),
            pl.BlockSpec(memory_space=pltpu.HBM),
        ]
        + [any_space] * 5,
        out_specs=pl.BlockSpec(memory_space=pltpu.VMEM),
        scratch_shapes=[
            pltpu.VMEM((sum(PIECES) * blk, width), jnp.bfloat16),
            pltpu.VMEM((rows, rounds, blk, blk), jnp.bfloat16),
            pltpu.SemaphoreType.DMA((5,)),
            pltpu.SemaphoreType.DMA((rows,)),
        ],
        compiler_params=pltpu.CompilerParams(vmem_limit_bytes=24 * 2**20),
        cost_estimate=pl.CostEstimate(
            flops=2 * rounds * rows * blk * blk * width, bytes_accessed=9 * 2**20, transcendentals=0
        ),
        name="panel_products",
    )(place, pltpu.with_memory_space_constraint(values, pltpu.HBM), *pieces)


def summed_over_rep(partial):
    received = lax.all_to_all(partial, REP, 0, 0, tiled=True)
    return jnp.sum(received.astype(jnp.float32), axis=0)


def dense_grads(hidden, weight, cotangent):
    pre_act = jnp.dot(hidden, weight, preferred_element_type=jnp.float32)
    sigmoid_value = jax.nn.sigmoid(pre_act)
    slope_value = sigmoid_value * (1.0 + pre_act * (1.0 - sigmoid_value))
    grad_pre = (cotangent.astype(jnp.float32) * slope_value).astype(jnp.bfloat16)
    hidden_grad = jnp.einsum(
        "rg,fg->rf", grad_pre, weight, preferred_element_type=jnp.float32
    ).astype(jnp.bfloat16)
    weight_part = jnp.einsum("rf,rg->fg", hidden, grad_pre, preferred_element_type=jnp.float32)
    return hidden_grad, weight_part


def shards(features, block_values, block_columns, weight, cotangent):
    values = block_values[0]
    rows, f = features.shape
    node_total = rows * lax.axis_size(AXES)
    inv_scale = 1.0 / math.sqrt(node_total)
    place = places(block_columns[0])
    panels, _ = gather_panels(features)
    partial = panel_products(values, place, panels)
    hidden = summed_over_rep(partial).astype(jnp.bfloat16)
    hidden_grad, weight_part = dense_grads(hidden, weight, cotangent)
    n_rep = lax.axis_size(REP)
    slices = lax.all_to_all(weight_part.reshape(n_rep, -1, f), REP, 0, 0, tiled=True)
    panels, weight_slice = gather_panels(hidden_grad, jnp.sum(slices, axis=0).astype(jnp.bfloat16))
    extra = weight_slice.shape[0]
    back = panel_products(values, place, panels, extra)
    back = back.at[:, rows:].set(weight_slice.astype(jnp.bfloat16)[None])
    received = lax.all_to_all(back, REP, 0, 0, tiled=True).astype(jnp.float32)
    feature_grad = jnp.sum(received[:, :rows], axis=0).astype(jnp.bfloat16)
    weight_grad = received[:, rows:].reshape(f, f) * inv_scale
    return feature_grad, weight_grad


def solution(mesh):
    finer = Mesh(mesh.devices.reshape(4, 4, 4, 4, 2), AXES)
    in_specs = (
        P(AXES, None),
        P(AXES, None, None, None, None),
        P(AXES, None, None),
        P(),
        P(AXES, None),
    )
    out_specs = (P(AXES, None), P())
    return jax.shard_map(
        shards, mesh=finer, in_specs=in_specs, out_specs=out_specs, check_vma=False
    )
```

```python
import math

import jax
import jax.numpy as jnp
from jax import lax
from jax.experimental import pallas as pl
from jax.experimental.pallas import tpu as pltpu
from jax.sharding import Mesh
from jax.sharding import PartitionSpec as P


AXES = ("X", "ZH", "ZL", "Y", "C")
DOM = ("X", "ZH", "ZL")
REP = ("Y", "C")
N_X, N_Z, FOUR = 4, 16, 4

SECOND = (((0, 2), (2, 1), (2, -1)), ((2, 0), (1, 2), (-1, -2)))
THIRD = (((1, 0), (-1, 0), (0, 1), (0, -1)), ((0, 1), (0, -1), (1, 0), (-1, 0)))
PIECES = (16, 16, 16, 8, 8)
BLK = 128


def place_table(core):
    held = ((0, 0),) + SECOND[core]
    table = {k: 4 * i for i, k in enumerate(held)}
    at = PIECES[0]
    for i, (dx, dz) in enumerate(THIRD[core]):
        sent = held if i < 2 else (held[0], held[2])
        for hx, hz in sent:
            table[(hx + dx, hz + dz)] = at
            at += 4
    flat = [None] * (N_X * FOUR)
    for (dx, dl), start in table.items():
        flat[dx % N_X * FOUR + dl % FOUR] = start
    return flat


def shift(value, first, second):
    pairs = []
    for x in range(N_X):
        for z in range(N_Z):
            for core, (dx, dz) in enumerate((first, second)):
                if (dx, dz) == (0, 2) and z % 2:
                    dz = -2
                source = (x + dx) % N_X * N_Z + (z + dz) % N_Z
                pairs.append((source * 2 + core, (x * N_Z + z) * 2 + core))
    return lax.ppermute(value, DOM + ("C",), pairs)


def halves(value):
    high = lax.reduce_precision(value, 8, 7)
    low = lax.reduce_precision(value - high, 8, 7)
    return jnp.concatenate([high, low], axis=-2).astype(jnp.bfloat16)


def whole(pair):
    high, low = jnp.split(pair.astype(jnp.float32), 2, axis=-2)
    return high + low


def gather_panels(value, riding=None):
    rows, width = value.shape

    def stacked(parts, pair):
        return jnp.concatenate(parts if pair is None else [*parts, pair], axis=0)

    got = lax.all_gather(stacked([value], riding), "ZH", axis=0, tiled=False)
    own = got[:, :rows].reshape(-1, width)
    size, pair = own.shape[0], None
    if riding is not None:
        pair = halves(jnp.sum(got[:, rows:].astype(jnp.float32), axis=0))
    packed = stacked([own], pair)
    more = []
    for steps in zip(*SECOND):
        more.append(shift(packed, *steps))
    if riding is not None:
        terms = [whole(pair)]
        for m in more:
            terms.append(whole(m[size:]))
        pair = halves((terms[0] + terms[1]) + (terms[2] + terms[3]))
    held = stacked([own] + [m[:size] for m in more], pair)
    half = jnp.concatenate(lax.optimization_barrier([own, more[1][:size]]), axis=0)
    near = []
    for i, steps in enumerate(zip(*THIRD)):
        sent = held if i < 2 else half if i == 2 else stacked([half], pair)
        near.append(shift(sent, *steps))
    total = None
    if riding is not None:
        n = pair.shape[0]
        plus, minus, side = (whole(near[i][-n:]) for i in (0, 1, 3))
        total = (whole(pair) + side) + (plus + minus)
    return (held, *near), total


def places(columns):
    cols = columns.T
    dx = (cols // N_Z - lax.axis_index("X")) % N_X
    dl = (cols - lax.axis_index("ZL")) % FOUR
    kind = dx * FOUR + dl
    core = lax.axis_index("C")
    base = jnp.zeros_like(cols)
    for k, (zero, one) in enumerate(zip(place_table(0), place_table(1))):
        base = jnp.where(kind == k, jnp.where(core == 0, zero, one), base)
    return (base + cols // FOUR % FOUR) * BLK


def product_kernel(place_ref, values_ref, *refs):
    pieces, (out_ref, panels, blocks, piece_sem, block_sem) = refs[:5], refs[5:]
    rows, rounds, blk, _ = blocks.shape
    copies = []
    for a in range(rows):
        copies.append(pltpu.make_async_copy(values_ref.at[:, a], blocks.at[a], block_sem.at[a]))
    moves, at = [], 0
    for i, piece in enumerate(pieces):
        n = PIECES[i] * blk
        moves.append(
            pltpu.make_async_copy(
                piece.at[pl.ds(0, n)], panels.at[pl.ds(at, n)], piece_sem.at[i]
            )
        )
        at += n
    for move in moves:
        move.start()
    for copy in copies:
        copy.start()
    for move in moves:
        move.wait()

    def panel(a, t):
        return panels[pl.ds(pl.multiple_of(place_ref[a, t], blk), blk)]

    for a in range(rows):
        copies[a].wait()
        total = None
        for t in range(0, rounds, 2):
            left = jnp.concatenate([blocks[a, t], blocks[a, t + 1]], axis=1)
            right = jnp.concatenate([panel(a, t), panel(a, t + 1)], axis=0)
            term = jnp.dot(left, right, preferred_element_type=jnp.float32)
            total = term if total is None else total + term
        out_ref[a, 0:blk] = total.astype(out_ref.dtype)


def panel_products(values, place, pieces, spare=0):
    rounds, rows, blk, _ = values.shape
    width = pieces[0].shape[-1]
    any_space = pl.BlockSpec(memory_space=pl.ANY)
    return pl.pallas_call(
        product_kernel,
        out_shape=jax.ShapeDtypeStruct((rows, blk + spare, width), jnp.bfloat16),
        in_specs=[
            pl.BlockSpec(memory_space=pltpu.SMEM),
            any_space,
        ]
        + [any_space] * 5,
        out_specs=pl.BlockSpec(memory_space=pltpu.VMEM),
        scratch_shapes=[
            pltpu.VMEM((sum(PIECES) * blk, width), jnp.bfloat16),
            pltpu.VMEM((rows, rounds, blk, blk), jnp.bfloat16),
            pltpu.SemaphoreType.DMA((5,)),
            pltpu.SemaphoreType.DMA((rows,)),
        ],
        compiler_params=pltpu.CompilerParams(vmem_limit_bytes=24 * 2**20),
        cost_estimate=pl.CostEstimate(
            flops=2 * rounds * rows * blk * blk * width, bytes_accessed=9 * 2**20, transcendentals=0
        ),
        name="panel_products",
    )(place, values, *pieces)


def summed_over_rep(partial):
    received = lax.all_to_all(partial, REP, 0, 0, tiled=True)
    return jnp.sum(received.astype(jnp.float32), axis=0)


def dense_grads(hidden, weight, cotangent):
    pre_act = jnp.dot(hidden, weight, preferred_element_type=jnp.float32)
    sigmoid_value = jax.nn.sigmoid(pre_act)
    slope_value = sigmoid_value * (1.0 + pre_act * (1.0 - sigmoid_value))
    grad_pre = (cotangent.astype(jnp.float32) * slope_value).astype(jnp.bfloat16)
    hidden_grad = jnp.einsum(
        "rg,fg->rf", grad_pre, weight, preferred_element_type=jnp.float32
    ).astype(jnp.bfloat16)
    weight_part = jnp.einsum("rf,rg->fg", hidden, grad_pre, preferred_element_type=jnp.float32)
    return hidden_grad, weight_part


def shards(features, block_values, block_columns, weight, cotangent):
    values = block_values[0]
    rows, f = features.shape
    node_total = rows * lax.axis_size(AXES)
    inv_scale = 1.0 / math.sqrt(node_total)
    place = places(block_columns[0])
    panels, _ = gather_panels(features)
    partial = panel_products(pltpu.with_memory_space_constraint(values, pltpu.HBM), place, panels)
    hidden = summed_over_rep(partial).astype(jnp.bfloat16)
    hidden_grad, weight_part = dense_grads(hidden, weight, cotangent)
    n_rep = lax.axis_size(REP)
    slices = lax.all_to_all(weight_part.reshape(n_rep, -1, f), REP, 0, 0, tiled=True)
    weight_slice = jnp.sum(slices, axis=0).astype(jnp.bfloat16)
    panels, weight_slice = gather_panels(hidden_grad, weight_slice)
    extra = weight_slice.shape[0]
    back = panel_products(values, place, panels, extra)
    back = back.at[:, rows:].set(weight_slice.astype(jnp.bfloat16)[None])
    received = lax.all_to_all(back, REP, 0, 0, tiled=True).astype(jnp.float32)
    feature_grad = jnp.sum(received[:, :rows], axis=0).astype(jnp.bfloat16)
    weight_grad = received[:, rows:].reshape(f, f) * inv_scale
    return feature_grad, weight_grad


def solution(mesh):
    finer = Mesh(mesh.devices.reshape(4, 4, 4, 4, 2), AXES)
    in_specs = (
        P(AXES, None),
        P(AXES, None, None, None, None),
        P(AXES, None, None),
        P(),
        P(AXES, None),
    )
    out_specs = (P(AXES, None), P())
    return jax.shard_map(
        shards, mesh=finer, in_specs=in_specs, out_specs=out_specs, check_vma=False
    )
```

```python
import math

import jax
import jax.numpy as jnp
from jax import lax
from jax.experimental import pallas as pl
from jax.experimental.pallas import tpu as pltpu
from jax.sharding import Mesh
from jax.sharding import PartitionSpec as P


AXES = ("X", "ZH", "ZL", "Y", "C")
DOM = ("X", "ZH", "ZL")
REP = ("Y", "C")
N_X, N_Z, FOUR = 4, 16, 4

SECOND = (((0, 2), (2, 1), (2, -1)), ((2, 0), (1, 2), (-1, -2)))
THIRD = (((1, 0), (-1, 0), (0, 1), (0, -1)), ((0, 1), (0, -1), (1, 0), (-1, 0)))
PIECES = (16, 16, 16, 8, 8)
BLK = 128


def place_table(core):
    held = ((0, 0),) + SECOND[core]
    table = {k: 4 * i for i, k in enumerate(held)}
    at = PIECES[0]
    for i, (dx, dz) in enumerate(THIRD[core]):
        sent = held if i < 2 else (held[0], held[2])
        for hx, hz in sent:
            table[(hx + dx, hz + dz)] = at
            at += 4
    flat = [None] * (N_X * FOUR)
    for (dx, dl), start in table.items():
        flat[dx % N_X * FOUR + dl % FOUR] = start
    return flat


def shift(value, first, second):
    pairs = []
    for x in range(N_X):
        for z in range(N_Z):
            for core, (dx, dz) in enumerate((first, second)):
                if (dx, dz) == (0, 2) and z % 2:
                    dz = -2
                source = (x + dx) % N_X * N_Z + (z + dz) % N_Z
                pairs.append((source * 2 + core, (x * N_Z + z) * 2 + core))
    return lax.ppermute(value, DOM + ("C",), pairs)


def halves(value):
    high = lax.reduce_precision(value, 8, 7)
    low = lax.reduce_precision(value - high, 8, 7)
    return jnp.concatenate([high, low], axis=-2).astype(jnp.bfloat16)


def whole(pair):
    high, low = jnp.split(pair.astype(jnp.float32), 2, axis=-2)
    return high + low


def gather_panels(value, riding=None):
    rows, width = value.shape

    def stacked(parts, pair):
        return jnp.concatenate(parts if pair is None else [*parts, pair], axis=0)

    got = lax.all_gather(stacked([value], riding), "ZH", axis=0, tiled=False)
    own = got[:, :rows].reshape(-1, width)
    size, pair = own.shape[0], None
    if riding is not None:
        pair = halves(jnp.sum(got[:, rows:].astype(jnp.float32), axis=0))
    packed = stacked([own], pair)
    more = []
    for steps in zip(*SECOND):
        more.append(shift(packed, *steps))
    if riding is not None:
        terms = [whole(pair)]
        for m in more:
            terms.append(whole(m[size:]))
        pair = halves((terms[0] + terms[1]) + (terms[2] + terms[3]))
    held = stacked([own] + [m[:size] for m in more], pair)
    half = jnp.concatenate(lax.optimization_barrier([own, more[1][:size]]), axis=0)
    near = []
    for i, steps in enumerate(zip(*THIRD)):
        sent = held if i < 2 else half if i == 2 else stacked([half], pair)
        near.append(shift(sent, *steps))
    total = None
    if riding is not None:
        n = pair.shape[0]
        plus, minus, side = (whole(near[i][-n:]) for i in (0, 1, 3))
        total = (whole(pair) + side) + (plus + minus)
    return (held, *near), total


def places(columns):
    cols = columns.T
    dx = (cols // N_Z - lax.axis_index("X")) % N_X
    dl = (cols - lax.axis_index("ZL")) % FOUR
    kind = dx * FOUR + dl
    core = lax.axis_index("C")
    base = jnp.zeros_like(cols)
    for k, (zero, one) in enumerate(zip(place_table(0), place_table(1))):
        base = jnp.where(kind == k, jnp.where(core == 0, zero, one), base)
    return (base + cols // FOUR % FOUR) * BLK


def load_kernel(values_ref, out_ref, sem):
    copy = pltpu.make_async_copy(values_ref, out_ref, sem)
    copy.start()
    copy.wait()


def loaded(values):
    return pl.pallas_call(
        load_kernel,
        out_shape=jax.ShapeDtypeStruct(values.shape, values.dtype),
        in_specs=[pl.BlockSpec(memory_space=pl.ANY)],
        out_specs=pl.BlockSpec(memory_space=pltpu.VMEM),
        scratch_shapes=[pltpu.SemaphoreType.DMA],
        compiler_params=pltpu.CompilerParams(vmem_limit_bytes=2**20),
        name="load_blocks",
    )(pltpu.with_memory_space_constraint(values, pltpu.HBM))


def product_kernel(place_ref, values_ref, *refs):
    pieces, (out_ref, panels, piece_sem) = refs[:5], refs[5:]
    rounds, rows, blk, _ = values_ref.shape
    moves, at = [], 0
    for i, piece in enumerate(pieces):
        n = PIECES[i] * blk
        moves.append(
            pltpu.make_async_copy(
                piece.at[pl.ds(0, n)], panels.at[pl.ds(at, n)], piece_sem.at[i]
            )
        )
        at += n
    for move in moves:
        move.start()
    for move in moves:
        move.wait()

    def panel(a, t):
        return panels[pl.ds(pl.multiple_of(place_ref[a, t], blk), blk)]

    for a in range(rows):
        total = None
        for t in range(0, rounds, 2):
            left = jnp.concatenate([values_ref[t, a], values_ref[t + 1, a]], axis=1)
            right = jnp.concatenate([panel(a, t), panel(a, t + 1)], axis=0)
            term = jnp.dot(left, right, preferred_element_type=jnp.float32)
            total = term if total is None else total + term
        out_ref[a, 0:blk] = total.astype(out_ref.dtype)


def panel_products(values, place, pieces, spare=0):
    rounds, rows, blk, _ = values.shape
    width = pieces[0].shape[-1]
    any_space = pl.BlockSpec(memory_space=pl.ANY)
    return pl.pallas_call(
        product_kernel,
        out_shape=jax.ShapeDtypeStruct((rows, blk + spare, width), jnp.bfloat16),
        in_specs=[
            pl.BlockSpec(memory_space=pltpu.SMEM),
            pl.BlockSpec(memory_space=pltpu.VMEM),
        ]
        + [any_space] * 5,
        out_specs=pl.BlockSpec(memory_space=pltpu.VMEM),
        scratch_shapes=[
            pltpu.VMEM((sum(PIECES) * blk, width), jnp.bfloat16),
            pltpu.SemaphoreType.DMA((5,)),
        ],
        compiler_params=pltpu.CompilerParams(vmem_limit_bytes=20 * 2**20),
        cost_estimate=pl.CostEstimate(
            flops=2 * rounds * rows * blk * blk * width, bytes_accessed=9 * 2**20, transcendentals=0
        ),
        name="panel_products",
    )(place, values, *pieces)


def summed_over_rep(partial):
    received = lax.all_to_all(partial, REP, 0, 0, tiled=True)
    return jnp.sum(received.astype(jnp.float32), axis=0)


def dense_grads(hidden, weight, cotangent):
    pre_act = jnp.dot(hidden, weight, preferred_element_type=jnp.float32)
    sigmoid_value = jax.nn.sigmoid(pre_act)
    slope_value = sigmoid_value * (1.0 + pre_act * (1.0 - sigmoid_value))
    grad_pre = (cotangent.astype(jnp.float32) * slope_value).astype(jnp.bfloat16)
    hidden_grad = jnp.einsum(
        "rg,fg->rf", grad_pre, weight, preferred_element_type=jnp.float32
    ).astype(jnp.bfloat16)
    weight_part = jnp.einsum("rf,rg->fg", hidden, grad_pre, preferred_element_type=jnp.float32)
    return hidden_grad, weight_part


def shards(features, block_values, block_columns, weight, cotangent):
    values = block_values[0]
    rows, f = features.shape
    node_total = rows * lax.axis_size(AXES)
    inv_scale = 1.0 / math.sqrt(node_total)
    place = places(block_columns[0])
    panels, _ = gather_panels(features)
    blocks = loaded(values)
    partial = panel_products(blocks, place, panels)
    hidden = summed_over_rep(partial).astype(jnp.bfloat16)
    hidden_grad, weight_part = dense_grads(hidden, weight, cotangent)
    n_rep = lax.axis_size(REP)
    weight_part = weight_part.astype(jnp.bfloat16).reshape(n_rep, -1, f)
    slices = lax.all_to_all(weight_part, REP, 0, 0, tiled=True)
    weight_slice = jnp.sum(slices.astype(jnp.float32), axis=0).astype(jnp.bfloat16)
    panels, weight_slice = gather_panels(hidden_grad, weight_slice)
    extra = weight_slice.shape[0]
    back = panel_products(values, place, panels, extra)
    back = back.at[:, rows:].set(weight_slice.astype(jnp.bfloat16)[None])
    received = lax.all_to_all(back, REP, 0, 0, tiled=True).astype(jnp.float32)
    feature_grad = jnp.sum(received[:, :rows], axis=0).astype(jnp.bfloat16)
    weight_grad = received[:, rows:].reshape(f, f) * inv_scale
    return feature_grad, weight_grad


def solution(mesh):
    finer = Mesh(mesh.devices.reshape(4, 4, 4, 4, 2), AXES)
    in_specs = (
        P(AXES, None),
        P(AXES, None, None, None, None),
        P(AXES, None, None),
        P(),
        P(AXES, None),
    )
    out_specs = (P(AXES, None), P())
    return jax.shard_map(
        shards, mesh=finer, in_specs=in_specs, out_specs=out_specs, check_vma=False
    )
```

```python
import functools
import math

import jax
import jax.numpy as jnp
from jax import lax
from jax.experimental import pallas as pl
from jax.experimental.pallas import tpu as pltpu
from jax.sharding import Mesh
from jax.sharding import PartitionSpec as P


AXES = ("X", "ZH", "ZL", "Y", "C")
DOM = ("X", "ZH", "ZL")
REP = ("Y", "C")
N_X, N_Z, FOUR = 4, 16, 4

SECOND = (((2, 1), (0, 2), (2, -1)), ((1, 2), (2, 0), (-1, -2)))
THIRD = (((1, 0), (-1, 0), (0, 1), (0, -1)), ((0, 1), (0, -1), (1, 0), (-1, 0)))
PIECES = (16, 16, 16, 8, 8)
BLK = 128


def place_table(core):
    held = ((0, 0),) + SECOND[core]
    table = {k: 4 * i for i, k in enumerate(held)}
    at = PIECES[0]
    for i, (dx, dz) in enumerate(THIRD[core]):
        sent = held if i < 2 else held[:2]
        for hx, hz in sent:
            table[(hx + dx, hz + dz)] = at
            at += 4
    flat = [None] * (N_X * FOUR)
    for (dx, dl), start in table.items():
        flat[dx % N_X * FOUR + dl % FOUR] = start
    return flat


def shift(value, first, second):
    pairs = []
    for x in range(N_X):
        for z in range(N_Z):
            for core, (dx, dz) in enumerate((first, second)):
                if (dx, dz) == (0, 2) and z % 2:
                    dz = -2
                source = (x + dx) % N_X * N_Z + (z + dz) % N_Z
                pairs.append((source * 2 + core, (x * N_Z + z) * 2 + core))
    return lax.ppermute(value, DOM + ("C",), pairs)


def halves(value):
    high = lax.reduce_precision(value, 8, 7)
    low = lax.reduce_precision(value - high, 8, 7)
    return jnp.concatenate([high, low], axis=-2).astype(jnp.bfloat16)


def whole(pair):
    high, low = jnp.split(pair.astype(jnp.float32), 2, axis=-2)
    return high + low


def gather_panels(value, riding=None):
    rows, width = value.shape

    def stacked(parts, pair):
        return jnp.concatenate(parts if pair is None else [*parts, pair], axis=0)

    got = lax.all_gather(stacked([value], riding), "ZH", axis=0, tiled=False)
    own = got[:, :rows].reshape(-1, width)
    size, pair = own.shape[0], None
    if riding is not None:
        pair = halves(jnp.sum(got[:, rows:].astype(jnp.float32), axis=0))
    packed = stacked([own], pair)
    more = []
    for steps in zip(*SECOND):
        more.append(shift(packed, *steps))
    if riding is not None:
        terms = [whole(pair)]
        for m in more:
            terms.append(whole(m[size:]))
        pair = halves((terms[0] + terms[2]) + (terms[1] + terms[3]))
    held = stacked([own] + [m[:size] for m in more], pair)
    half = jnp.concatenate(lax.optimization_barrier([own, more[0][:size]]), axis=0)
    near = []
    for i, steps in enumerate(zip(*THIRD)):
        near.append(shift(held if i < 2 else half, *steps))
    total = None
    if riding is not None:
        side = whole(shift(pair, *list(zip(*THIRD))[2]))
        n = pair.shape[0]
        plus, minus = (whole(v[-n:]) for v in near[:2])
        total = (whole(pair) + side) + (plus + minus)
    return (held, *near), total


def places(columns):
    cols = columns.T
    dx = (cols // N_Z - lax.axis_index("X")) % N_X
    dl = (cols - lax.axis_index("ZL")) % FOUR
    kind = dx * FOUR + dl
    core = lax.axis_index("C")
    base = jnp.zeros_like(cols)
    for k, (zero, one) in enumerate(zip(place_table(0), place_table(1))):
        base = jnp.where(kind == k, jnp.where(core == 0, zero, one), base)
    return (base + cols // FOUR % FOUR) * BLK


def load_kernel(values_ref, out_ref, sem):
    copy = pltpu.make_async_copy(values_ref, out_ref, sem)
    copy.start()
    copy.wait()


def loaded(values):
    return pl.pallas_call(
        load_kernel,
        out_shape=jax.ShapeDtypeStruct(values.shape, values.dtype),
        in_specs=[pl.BlockSpec(memory_space=pl.ANY)],
        out_specs=pl.BlockSpec(memory_space=pltpu.VMEM),
        scratch_shapes=[pltpu.SemaphoreType.DMA],
        compiler_params=pltpu.CompilerParams(vmem_limit_bytes=2**20),
        name="load_blocks",
    )(pltpu.with_memory_space_constraint(values, pltpu.HBM))


def product_kernel(place_ref, values_ref, *refs):
    pieces, (out_ref, panels, piece_sem) = refs[:5], refs[5:]
    rounds, rows, blk, _ = values_ref.shape
    moves, at = [], 0
    for i, piece in enumerate(pieces):
        n = PIECES[i] * blk
        moves.append(
            pltpu.make_async_copy(
                piece.at[pl.ds(0, n)], panels.at[pl.ds(at, n)], piece_sem.at[i]
            )
        )
        at += n
    for move in moves:
        move.start()
    for move in moves:
        move.wait()

    def panel(a, t):
        return panels[pl.ds(pl.multiple_of(place_ref[a, t], blk), blk)]

    for a in range(rows):
        total = None
        for t in range(0, rounds, 2):
            left = jnp.concatenate([values_ref[t, a], values_ref[t + 1, a]], axis=1)
            right = jnp.concatenate([panel(a, t), panel(a, t + 1)], axis=0)
            term = jnp.dot(left, right, preferred_element_type=jnp.float32)
            total = term if total is None else total + term
        out_ref[a, 0:blk] = total.astype(out_ref.dtype)


def panel_products(values, place, pieces, spare=0):
    rounds, rows, blk, _ = values.shape
    width = pieces[0].shape[-1]
    any_space = pl.BlockSpec(memory_space=pl.ANY)
    return pl.pallas_call(
        product_kernel,
        out_shape=jax.ShapeDtypeStruct((rows, blk + spare, width), jnp.bfloat16),
        in_specs=[
            pl.BlockSpec(memory_space=pltpu.SMEM),
            pl.BlockSpec(memory_space=pltpu.VMEM),
        ]
        + [any_space] * 5,
        out_specs=pl.BlockSpec(memory_space=pltpu.VMEM),
        scratch_shapes=[
            pltpu.VMEM((sum(PIECES) * blk, width), jnp.bfloat16),
            pltpu.SemaphoreType.DMA((5,)),
        ],
        compiler_params=pltpu.CompilerParams(vmem_limit_bytes=20 * 2**20),
        cost_estimate=pl.CostEstimate(
            flops=2 * rounds * rows * blk * blk * width, bytes_accessed=9 * 2**20, transcendentals=0
        ),
        name="panel_products",
    )(place, values, *pieces)


def summed_over_rep(partial):
    received = lax.all_to_all(partial, REP, 0, 0, tiled=True)
    return jnp.sum(received.astype(jnp.float32), axis=0)


def tail_kernel(scale, received_ref, sum_ref, slice_ref):
    rows = sum_ref.shape[0]
    total = received_ref[0, 0:rows].astype(jnp.float32)
    for i in range(1, received_ref.shape[0]):
        total = total + received_ref[i, 0:rows].astype(jnp.float32)
    sum_ref[...] = total.astype(sum_ref.dtype)
    for i in range(received_ref.shape[0]):
        slice_ref[i] = received_ref[i, rows:].astype(jnp.float32) * scale


def tail(received, rows, scale):
    n, high, width = received.shape
    return pl.pallas_call(
        functools.partial(tail_kernel, scale),
        out_shape=(
            jax.ShapeDtypeStruct((rows, width), jnp.bfloat16),
            jax.ShapeDtypeStruct((n, high - rows, width), jnp.float32),
        ),
        in_specs=[pl.BlockSpec(memory_space=pltpu.VMEM)],
        out_specs=(pl.BlockSpec(memory_space=pltpu.VMEM),) * 2,
        compiler_params=pltpu.CompilerParams(vmem_limit_bytes=8 * 2**20),
        name="tail",
    )(received)


def dense_grads(hidden, weight, cotangent):
    pre_act = jnp.dot(hidden, weight, preferred_element_type=jnp.float32)
    sigmoid_value = jax.nn.sigmoid(pre_act)
    slope_value = sigmoid_value * (1.0 + pre_act * (1.0 - sigmoid_value))
    grad_pre = (cotangent.astype(jnp.float32) * slope_value).astype(jnp.bfloat16)
    hidden_grad = jnp.einsum(
        "rg,fg->rf", grad_pre, weight, preferred_element_type=jnp.float32
    ).astype(jnp.bfloat16)
    weight_part = jnp.einsum("rf,rg->fg", hidden, grad_pre, preferred_element_type=jnp.float32)
    return hidden_grad, weight_part


def shards(features, block_values, block_columns, weight, cotangent):
    values = block_values[0]
    rows, f = features.shape
    node_total = rows * lax.axis_size(AXES)
    inv_scale = 1.0 / math.sqrt(node_total)
    place = places(block_columns[0])
    panels, _ = gather_panels(features)
    blocks = loaded(values)
    partial = panel_products(blocks, place, panels)
    hidden = summed_over_rep(partial).astype(jnp.bfloat16)
    hidden_grad, weight_part = dense_grads(hidden, weight, cotangent)
    n_rep = lax.axis_size(REP)
    weight_part = weight_part.astype(jnp.bfloat16).reshape(n_rep, -1, f)
    slices = lax.all_to_all(weight_part, REP, 0, 0, tiled=True)
    weight_slice = jnp.sum(slices.astype(jnp.float32), axis=0).astype(jnp.bfloat16)
    panels, weight_slice = gather_panels(hidden_grad, weight_slice)
    extra = weight_slice.shape[0]
    back = panel_products(values, place, panels, extra)
    back = back.at[:, rows:].set(weight_slice.astype(jnp.bfloat16)[None])
    received = lax.all_to_all(back, REP, 0, 0, tiled=True)
    feature_grad, weight_grad = tail(received, rows, inv_scale)
    return feature_grad, weight_grad.reshape(f, f)


def solution(mesh):
    finer = Mesh(mesh.devices.reshape(4, 4, 4, 4, 2), AXES)
    in_specs = (
        P(AXES, None),
        P(AXES, None, None, None, None),
        P(AXES, None, None),
        P(),
        P(AXES, None),
    )
    out_specs = (P(AXES, None), P())
    return jax.shard_map(
        shards, mesh=finer, in_specs=in_specs, out_specs=out_specs, check_vma=False
    )
```

```python
import functools
import math

import jax
import jax.numpy as jnp
from jax import lax
from jax.experimental import pallas as pl
from jax.experimental.pallas import tpu as pltpu
from jax.sharding import Mesh
from jax.sharding import PartitionSpec as P


AXES = ("X", "ZH", "ZL", "Y", "C")
DOM = ("X", "ZH", "ZL")
REP = ("Y", "C")
N_X, N_Z, FOUR = 4, 16, 4

SECOND = (((2, 1), (0, 2), (2, -1)), ((1, 2), (2, 0), (-1, -2)))
THIRD = (((1, 0), (-1, 0), (0, 1), (0, -1)), ((0, 1), (0, -1), (1, 0), (-1, 0)))
PIECES, EACH = 8, 8
BLK = 128


def place_table(core):
    held = ((0, 0),) + SECOND[core]
    table = {k: 4 * i for i, k in enumerate(held)}
    at = 4 * len(held)
    for i, (dx, dz) in enumerate(THIRD[core]):
        sent = held if i < 2 else held[:2]
        for hx, hz in sent:
            table[(hx + dx, hz + dz)] = at
            at += 4
    flat = [None] * (N_X * FOUR)
    for (dx, dl), start in table.items():
        flat[dx % N_X * FOUR + dl % FOUR] = start
    return flat


def shift(value, first, second):
    pairs = []
    for x in range(N_X):
        for z in range(N_Z):
            for core, (dx, dz) in enumerate((first, second)):
                if (dx, dz) == (0, 2) and z % 2:
                    dz = -2
                source = (x + dx) % N_X * N_Z + (z + dz) % N_Z
                pairs.append((source * 2 + core, (x * N_Z + z) * 2 + core))
    return lax.ppermute(value, DOM + ("C",), pairs)


def halves(value):
    high = lax.reduce_precision(value, 8, 7)
    low = lax.reduce_precision(value - high, 8, 7)
    return jnp.concatenate([high, low], axis=-2).astype(jnp.bfloat16)


def whole(pair):
    high, low = jnp.split(pair.astype(jnp.float32), 2, axis=-2)
    return high + low


def gather_panels(value, riding=None):
    rows, width = value.shape

    def stacked(parts, pair):
        return jnp.concatenate(parts if pair is None else [*parts, pair], axis=0)

    got = lax.all_gather(stacked([value], riding), "ZH", axis=0, tiled=False)
    own = got[:, :rows].reshape(-1, width)
    size, pair = own.shape[0], None
    if riding is not None:
        pair = halves(jnp.sum(got[:, rows:].astype(jnp.float32), axis=0))
    packed = stacked([own], pair)
    more = []
    for steps in zip(*SECOND):
        more.append(shift(packed, *steps))
    if riding is not None:
        terms = [whole(pair)]
        for m in more:
            terms.append(whole(m[size:]))
        pair = halves((terms[0] + terms[2]) + (terms[1] + terms[3]))
    early = jnp.concatenate(lax.optimization_barrier([own, more[0][:size]]), axis=0)
    late = stacked([m[:size] for m in more[1:]], pair)
    near, rest = [], []
    for steps in zip(*THIRD):
        near.append(shift(early, *steps))
    for steps in list(zip(*THIRD))[:2]:
        rest.append(shift(late, *steps))
    total = None
    if riding is not None:
        side = whole(shift(pair, *list(zip(*THIRD))[2]))
        n = pair.shape[0]
        plus, minus = (whole(v[-n:]) for v in rest)
        total = (whole(pair) + side) + (plus + minus)
    return (early, late, near[0], rest[0], near[1], rest[1], *near[2:]), total


def places(columns):
    cols = columns.T
    dx = (cols // N_Z - lax.axis_index("X")) % N_X
    dl = (cols - lax.axis_index("ZL")) % FOUR
    kind = dx * FOUR + dl
    core = lax.axis_index("C")
    base = jnp.zeros_like(cols)
    for k, (zero, one) in enumerate(zip(place_table(0), place_table(1))):
        base = jnp.where(kind == k, jnp.where(core == 0, zero, one), base)
    return (base + cols // FOUR % FOUR) * BLK


def load_kernel(values_ref, out_ref, sem):
    copy = pltpu.make_async_copy(values_ref, out_ref, sem)
    copy.start()
    copy.wait()


def loaded(values):
    return pl.pallas_call(
        load_kernel,
        out_shape=jax.ShapeDtypeStruct(values.shape, values.dtype),
        in_specs=[pl.BlockSpec(memory_space=pl.ANY)],
        out_specs=pl.BlockSpec(memory_space=pltpu.VMEM),
        scratch_shapes=[pltpu.SemaphoreType.DMA],
        compiler_params=pltpu.CompilerParams(vmem_limit_bytes=2**20),
        name="load_blocks",
    )(pltpu.with_memory_space_constraint(values, pltpu.HBM))


def product_kernel(place_ref, values_ref, *refs):
    pieces, (out_ref, panels, piece_sem) = refs[:PIECES], refs[PIECES:]
    rounds, rows, blk, _ = values_ref.shape
    moves, n = [], EACH * blk
    for i, piece in enumerate(pieces):
        moves.append(
            pltpu.make_async_copy(
                piece.at[pl.ds(0, n)], panels.at[pl.ds(i * n, n)], piece_sem.at[i]
            )
        )
    for move in moves:
        move.start()
    for move in moves:
        move.wait()

    def panel(a, t):
        return panels[pl.ds(pl.multiple_of(place_ref[a, t], blk), blk)]

    for a in range(rows):
        total = None
        for t in range(0, rounds, 2):
            left = jnp.concatenate([values_ref[t, a], values_ref[t + 1, a]], axis=1)
            right = jnp.concatenate([panel(a, t), panel(a, t + 1)], axis=0)
            term = jnp.dot(left, right, preferred_element_type=jnp.float32)
            total = term if total is None else total + term
        out_ref[a, 0:blk] = total.astype(out_ref.dtype)


def panel_products(values, place, pieces, spare=0):
    rounds, rows, blk, _ = values.shape
    width = pieces[0].shape[-1]
    any_space = pl.BlockSpec(memory_space=pl.ANY)
    return pl.pallas_call(
        product_kernel,
        out_shape=jax.ShapeDtypeStruct((rows, blk + spare, width), jnp.bfloat16),
        in_specs=[
            pl.BlockSpec(memory_space=pltpu.SMEM),
            pl.BlockSpec(memory_space=pltpu.VMEM),
        ]
        + [any_space] * PIECES,
        out_specs=pl.BlockSpec(memory_space=pltpu.VMEM),
        scratch_shapes=[
            pltpu.VMEM((PIECES * EACH * blk, width), jnp.bfloat16),
            pltpu.SemaphoreType.DMA((PIECES,)),
        ],
        compiler_params=pltpu.CompilerParams(vmem_limit_bytes=20 * 2**20),
        cost_estimate=pl.CostEstimate(
            flops=2 * rounds * rows * blk * blk * width, bytes_accessed=9 * 2**20, transcendentals=0
        ),
        name="panel_products",
    )(place, values, *pieces)


def summed_over_rep(partial):
    received = lax.all_to_all(partial, REP, 0, 0, tiled=True)
    return jnp.sum(received.astype(jnp.float32), axis=0)


def tail_kernel(scale, received_ref, sum_ref, slice_ref):
    rows = sum_ref.shape[0]
    total = received_ref[0, 0:rows].astype(jnp.float32)
    for i in range(1, received_ref.shape[0]):
        total = total + received_ref[i, 0:rows].astype(jnp.float32)
    sum_ref[...] = total.astype(sum_ref.dtype)
    for i in range(received_ref.shape[0]):
        slice_ref[i] = received_ref[i, rows:].astype(jnp.float32) * scale


def tail(received, rows, scale):
    n, high, width = received.shape
    return pl.pallas_call(
        functools.partial(tail_kernel, scale),
        out_shape=(
            jax.ShapeDtypeStruct((rows, width), jnp.bfloat16),
            jax.ShapeDtypeStruct((n, high - rows, width), jnp.float32),
        ),
        in_specs=[pl.BlockSpec(memory_space=pltpu.VMEM)],
        out_specs=(pl.BlockSpec(memory_space=pltpu.VMEM),) * 2,
        compiler_params=pltpu.CompilerParams(vmem_limit_bytes=8 * 2**20),
        name="tail",
    )(received)


def dense_grads(hidden, weight, cotangent):
    pre_act = jnp.dot(hidden, weight, preferred_element_type=jnp.float32)
    sigmoid_value = jax.nn.sigmoid(pre_act)
    slope_value = sigmoid_value * (1.0 + pre_act * (1.0 - sigmoid_value))
    grad_pre = (cotangent.astype(jnp.float32) * slope_value).astype(jnp.bfloat16)
    hidden_grad = jnp.einsum(
        "rg,fg->rf", grad_pre, weight, preferred_element_type=jnp.float32
    ).astype(jnp.bfloat16)
    weight_part = jnp.einsum("rf,rg->fg", hidden, grad_pre, preferred_element_type=jnp.float32)
    return hidden_grad, weight_part


def shards(features, block_values, block_columns, weight, cotangent):
    values = block_values[0]
    rows, f = features.shape
    node_total = rows * lax.axis_size(AXES)
    inv_scale = 1.0 / math.sqrt(node_total)
    place = places(block_columns[0])
    panels, _ = gather_panels(features)
    blocks = loaded(values)
    partial = panel_products(blocks, place, panels)
    hidden = summed_over_rep(partial).astype(jnp.bfloat16)
    hidden_grad, weight_part = dense_grads(hidden, weight, cotangent)
    n_rep = lax.axis_size(REP)
    weight_part = weight_part.astype(jnp.bfloat16).reshape(n_rep, -1, f)
    slices = lax.all_to_all(weight_part, REP, 0, 0, tiled=True)
    weight_slice = jnp.sum(slices.astype(jnp.float32), axis=0).astype(jnp.bfloat16)
    panels, weight_slice = gather_panels(hidden_grad, weight_slice)
    extra = weight_slice.shape[0]
    back = panel_products(values, place, panels, extra)
    back = back.at[:, rows:].set(weight_slice.astype(jnp.bfloat16)[None])
    received = lax.all_to_all(back, REP, 0, 0, tiled=True)
    feature_grad, weight_grad = tail(received, rows, inv_scale)
    return feature_grad, weight_grad.reshape(f, f)


def solution(mesh):
    finer = Mesh(mesh.devices.reshape(4, 4, 4, 4, 2), AXES)
    in_specs = (
        P(AXES, None),
        P(AXES, None, None, None, None),
        P(AXES, None, None),
        P(),
        P(AXES, None),
    )
    out_specs = (P(AXES, None), P())
    return jax.shard_map(
        shards, mesh=finer, in_specs=in_specs, out_specs=out_specs, check_vma=False
    )
```

```python
import functools
import math

import jax
import jax.numpy as jnp
from jax import lax
from jax.experimental import pallas as pl
from jax.experimental.pallas import tpu as pltpu
from jax.sharding import Mesh
from jax.sharding import PartitionSpec as P


AXES = ("X", "ZH", "ZL", "Y", "C")
DOM = ("X", "ZH", "ZL")
REP = ("Y", "C")
N_X, N_Z, FOUR = 4, 16, 4

SECOND = (((2, 1), (0, 2), (2, -1)), ((1, 2), (2, 0), (-1, -2)))
THIRD = (((1, 0), (-1, 0), (0, 1), (0, -1)), ((0, 1), (0, -1), (1, 0), (-1, 0)))
SPLIT, JOINED = (8,) * 8, (16, 16, 16, 8, 8)
BLK = 128


def place_table(core):
    held = ((0, 0),) + SECOND[core]
    table = {k: 4 * i for i, k in enumerate(held)}
    at = 4 * len(held)
    for i, (dx, dz) in enumerate(THIRD[core]):
        sent = held if i < 2 else held[:2]
        for hx, hz in sent:
            table[(hx + dx, hz + dz)] = at
            at += 4
    flat = [None] * (N_X * FOUR)
    for (dx, dl), start in table.items():
        flat[dx % N_X * FOUR + dl % FOUR] = start
    return flat


def shift(value, first, second):
    pairs = []
    for x in range(N_X):
        for z in range(N_Z):
            for core, (dx, dz) in enumerate((first, second)):
                if (dx, dz) == (0, 2) and z % 2:
                    dz = -2
                source = (x + dx) % N_X * N_Z + (z + dz) % N_Z
                pairs.append((source * 2 + core, (x * N_Z + z) * 2 + core))
    return lax.ppermute(value, DOM + ("C",), pairs)


def halves(value):
    high = lax.reduce_precision(value, 8, 7)
    low = lax.reduce_precision(value - high, 8, 7)
    return jnp.concatenate([high, low], axis=-2).astype(jnp.bfloat16)


def whole(pair):
    high, low = jnp.split(pair.astype(jnp.float32), 2, axis=-2)
    return high + low


def gather_panels(value, riding=None):
    rows, width = value.shape

    def stacked(parts, pair):
        return jnp.concatenate(parts if pair is None else [*parts, pair], axis=0)

    got = lax.all_gather(stacked([value], riding), "ZH", axis=0, tiled=False)
    own = got[:, :rows].reshape(-1, width)
    size, pair = own.shape[0], None
    if riding is not None:
        pair = halves(jnp.sum(got[:, rows:].astype(jnp.float32), axis=0))
    packed = stacked([own], pair)
    more = []
    for steps in zip(*SECOND):
        more.append(shift(packed, *steps))
    if riding is not None:
        terms = [whole(pair)]
        for m in more:
            terms.append(whole(m[size:]))
        pair = halves((terms[0] + terms[2]) + (terms[1] + terms[3]))
    early = jnp.concatenate(lax.optimization_barrier([own, more[0][:size]]), axis=0)
    parts = [m[:size] for m in more]
    late = stacked(parts[1:] if riding is None else [own, *parts], pair)
    large = early if riding is None else late
    near, rest = [], []
    for i, steps in enumerate(zip(*THIRD)):
        near.append(shift(large if i < 2 else early, *steps))
    if riding is None:
        for steps in list(zip(*THIRD))[:2]:
            rest.append(shift(late, *steps))
        return (early, late, near[0], rest[0], near[1], rest[1], *near[2:]), None
    side = whole(shift(pair, *list(zip(*THIRD))[2]))
    n = pair.shape[0]
    plus, minus = (whole(v[-n:]) for v in near[:2])
    return (late, *near), (whole(pair) + side) + (plus + minus)


def places(columns):
    cols = columns.T
    dx = (cols // N_Z - lax.axis_index("X")) % N_X
    dl = (cols - lax.axis_index("ZL")) % FOUR
    kind = dx * FOUR + dl
    core = lax.axis_index("C")
    base = jnp.zeros_like(cols)
    for k, (zero, one) in enumerate(zip(place_table(0), place_table(1))):
        base = jnp.where(kind == k, jnp.where(core == 0, zero, one), base)
    return (base + cols // FOUR % FOUR) * BLK


def load_kernel(values_ref, out_ref, sem):
    copy = pltpu.make_async_copy(values_ref, out_ref, sem)
    copy.start()
    copy.wait()


def loaded(values):
    return pl.pallas_call(
        load_kernel,
        out_shape=jax.ShapeDtypeStruct(values.shape, values.dtype),
        in_specs=[pl.BlockSpec(memory_space=pl.ANY)],
        out_specs=pl.BlockSpec(memory_space=pltpu.VMEM),
        scratch_shapes=[pltpu.SemaphoreType.DMA],
        compiler_params=pltpu.CompilerParams(vmem_limit_bytes=2**20),
        name="load_blocks",
    )(pltpu.with_memory_space_constraint(values, pltpu.HBM))


def product_kernel(sizes, place_ref, values_ref, *refs):
    pieces, (out_ref, panels, piece_sem) = refs[: len(sizes)], refs[len(sizes) :]
    rounds, rows, blk, _ = values_ref.shape
    moves, at = [], 0
    for i, piece in enumerate(pieces):
        n = sizes[i] * blk
        moves.append(
            pltpu.make_async_copy(
                piece.at[pl.ds(0, n)], panels.at[pl.ds(at, n)], piece_sem.at[i]
            )
        )
        at += n
    for move in moves:
        move.start()
    for move in moves:
        move.wait()

    def panel(a, t):
        return panels[pl.ds(pl.multiple_of(place_ref[a, t], blk), blk)]

    for a in range(rows):
        total = None
        for t in range(0, rounds, 2):
            left = jnp.concatenate([values_ref[t, a], values_ref[t + 1, a]], axis=1)
            right = jnp.concatenate([panel(a, t), panel(a, t + 1)], axis=0)
            term = jnp.dot(left, right, preferred_element_type=jnp.float32)
            total = term if total is None else total + term
        out_ref[a, 0:blk] = total.astype(out_ref.dtype)


def panel_products(values, place, pieces, sizes, spare=0):
    rounds, rows, blk, _ = values.shape
    width = pieces[0].shape[-1]
    any_space = pl.BlockSpec(memory_space=pl.ANY)
    return pl.pallas_call(
        functools.partial(product_kernel, sizes),
        out_shape=jax.ShapeDtypeStruct((rows, blk + spare, width), jnp.bfloat16),
        in_specs=[
            pl.BlockSpec(memory_space=pltpu.SMEM),
            pl.BlockSpec(memory_space=pltpu.VMEM),
        ]
        + [any_space] * len(sizes),
        out_specs=pl.BlockSpec(memory_space=pltpu.VMEM),
        scratch_shapes=[
            pltpu.VMEM((sum(sizes) * blk, width), jnp.bfloat16),
            pltpu.SemaphoreType.DMA((len(sizes),)),
        ],
        compiler_params=pltpu.CompilerParams(vmem_limit_bytes=20 * 2**20),
        cost_estimate=pl.CostEstimate(
            flops=2 * rounds * rows * blk * blk * width, bytes_accessed=9 * 2**20, transcendentals=0
        ),
        name="panel_products",
    )(place, values, *pieces)


def summed_over_rep(partial):
    received = lax.all_to_all(partial, REP, 0, 0, tiled=True)
    return jnp.sum(received.astype(jnp.float32), axis=0)


def tail_kernel(scale, received_ref, sum_ref, slice_ref):
    rows = sum_ref.shape[0]
    total = received_ref[0, 0:rows].astype(jnp.float32)
    for i in range(1, received_ref.shape[0]):
        total = total + received_ref[i, 0:rows].astype(jnp.float32)
    sum_ref[...] = total.astype(sum_ref.dtype)
    for i in range(received_ref.shape[0]):
        slice_ref[i] = received_ref[i, rows:].astype(jnp.float32) * scale


def tail(received, rows, scale):
    n, high, width = received.shape
    return pl.pallas_call(
        functools.partial(tail_kernel, scale),
        out_shape=(
            jax.ShapeDtypeStruct((rows, width), jnp.bfloat16),
            jax.ShapeDtypeStruct((n, high - rows, width), jnp.float32),
        ),
        in_specs=[pl.BlockSpec(memory_space=pltpu.VMEM)],
        out_specs=(pl.BlockSpec(memory_space=pltpu.VMEM),) * 2,
        compiler_params=pltpu.CompilerParams(vmem_limit_bytes=8 * 2**20),
        name="tail",
    )(received)


def dense_grads(hidden, weight, cotangent):
    pre_act = jnp.dot(hidden, weight, preferred_element_type=jnp.float32)
    sigmoid_value = jax.nn.sigmoid(pre_act)
    slope_value = sigmoid_value * (1.0 + pre_act * (1.0 - sigmoid_value))
    grad_pre = (cotangent.astype(jnp.float32) * slope_value).astype(jnp.bfloat16)
    hidden_grad = jnp.einsum(
        "rg,fg->rf", grad_pre, weight, preferred_element_type=jnp.float32
    ).astype(jnp.bfloat16)
    weight_part = jnp.einsum("rf,rg->fg", hidden, grad_pre, preferred_element_type=jnp.float32)
    return hidden_grad, weight_part


def shards(features, block_values, block_columns, weight, cotangent):
    values = block_values[0]
    rows, f = features.shape
    node_total = rows * lax.axis_size(AXES)
    inv_scale = 1.0 / math.sqrt(node_total)
    place = places(block_columns[0])
    panels, _ = gather_panels(features)
    blocks = loaded(values)
    partial = panel_products(blocks, place, panels, SPLIT)
    hidden = summed_over_rep(partial).astype(jnp.bfloat16)
    hidden_grad, weight_part = dense_grads(hidden, weight, cotangent)
    n_rep = lax.axis_size(REP)
    weight_part = weight_part.astype(jnp.bfloat16).reshape(n_rep, -1, f)
    slices = lax.all_to_all(weight_part, REP, 0, 0, tiled=True)
    weight_slice = jnp.sum(slices.astype(jnp.float32), axis=0).astype(jnp.bfloat16)
    panels, weight_slice = gather_panels(hidden_grad, weight_slice)
    extra = weight_slice.shape[0]
    back = panel_products(values, place, panels, JOINED, extra)
    back = back.at[:, rows:].set(weight_slice.astype(jnp.bfloat16)[None])
    received = lax.all_to_all(back, REP, 0, 0, tiled=True)
    feature_grad, weight_grad = tail(received, rows, inv_scale)
    return feature_grad, weight_grad.reshape(f, f)


def solution(mesh):
    finer = Mesh(mesh.devices.reshape(4, 4, 4, 4, 2), AXES)
    in_specs = (
        P(AXES, None),
        P(AXES, None, None, None, None),
        P(AXES, None, None),
        P(),
        P(AXES, None),
    )
    out_specs = (P(AXES, None), P())
    return jax.shard_map(
        shards, mesh=finer, in_specs=in_specs, out_specs=out_specs, check_vma=False
    )
```
